32 devices in a mesh: expert: 8 (over y, x, core), tensor: 4 (over z).
Axes of the slice: x: 2, y: 2, z: 4, core: 2. Of those that a mesh axis runs over, the one named last changes fastest.
Arguments:
- grad_out: bfloat16 [1024, 4096], P('expert', 'tensor'), may hold values from -6 to 6
- expert_ids: int32 [1024, 4], P('expert'), may hold values from 0 to 7, all different within a row
- gate_probs: float32 [1024, 4], P('expert'), may hold values from 0.05 to 0.6
- live: int32 [1024], P('expert'), may hold values 0 or 1
- w_gate: bfloat16 [8, 5376, 4096], P('expert', 'tensor'), may hold values from -0.09375 to 0.09375
- w_up: bfloat16 [8, 5376, 4096], P('expert', 'tensor'), may hold values from -0.09375 to 0.09375
- w_down: bfloat16 [8, 5376, 4096], P('expert', 'tensor'), may hold values from -0.078125 to 0.078125
- saved: bfloat16 [8, 2, 5376, 512], P('expert', None, 'tensor'), may hold values from -8 to 8
Outputs:
- grad_in: bfloat16 [1024, 4096], P('expert', 'tensor')
The draws below stay inside these ranges and needn't reach their ends.
Inputs may be any that keep to these rules, and one draw needn't show every extreme that they name: `expert_ids`: the 4 ids of a token are different.
All inputs are finite; a program needn't handle non-finite values. No bound on the sum of `live` on one device may be relied on, other than what follows from the above.
Results may differ from the reference program's by a relative error of at most 0.012.
Values may be sent and summed in bfloat16 or wider, within the bound.
A program may use at most 128 MiB of HBM per device.

```python
import math
import jax
import jax.numpy as jnp
from jax import lax

D = 4096
FF = 5376
TOP = 4
TOK_G = 128
TOKENS = 1024
EXPERTS = 8
CAP = 64
SLOTS = 512
N_EXPERT = 8
N_TENSOR = 4


def place_ends(array, own_key, low, top_value):
    longest = array.shape.index(max(array.shape))
    spots = []
    for shift in (0, 1):
        where = [jax.random.randint(jax.random.fold_in(own_key, axis), (), 0, length) for axis, length in enumerate(array.shape)]
        where[longest] = (where[longest] + shift) % array.shape[longest]
        spots.append(tuple(where))
    return array.at[spots[0]].set(low).at[spots[1]].set(top_value)


def level_of(stream_key, dims, cuts, least, largest):
    gain, own = 1.0, jax.random.fold_in(stream_key, 6)
    for dim, blocks in cuts:
        steps = jnp.exp(jax.random.uniform(jax.random.fold_in(own, dim), (blocks,), jnp.float32, least / len(cuts), largest / len(cuts)))
        gain = gain * jnp.repeat(steps, dims[dim] // blocks).reshape([-1 if axis == dim else 1 for axis in range(len(dims))])
    return gain


def distinct(stream_key, rows, number_of, top, lift):
    ranking = jax.random.permutation(jax.random.fold_in(stream_key, 1), number_of)
    pull = ranking
    for power in range(3):
        pull = pull * pull // number_of
    pull = pull * lift // number_of
    tickets = jax.random.randint(jax.random.fold_in(stream_key, 2), (rows, number_of), 0, 4096) + pull
    sure = jax.random.permutation(jax.random.fold_in(stream_key, 3), rows)[jnp.arange(number_of) % rows]
    tickets = jnp.where(jnp.arange(rows)[:, None] == sure[None, :], 1 << 14, tickets)
    merit = tickets * number_of + jnp.arange(number_of)
    return lax.top_k(merit.astype(jnp.int32), top)[1].astype(jnp.int32)


def scatter_about(own_key, shape, spread, most, split=(), kind=jnp.bfloat16):
    drawn = jax.random.normal(own_key, shape, jnp.float32) * spread
    if len(split) > 0:
        drawn = level_of(own_key, shape, split, -0.22, 0.18) * drawn
    return jnp.clip(drawn, min=-most, max=most).astype(kind)


def setup_inputs(seed: int = 0) -> dict:
    streams_of = jax.random.split(jax.random.key(seed), 9)
    return {
        "grad_out": scatter_about(streams_of[0], (TOKENS, D), 1.0, 6.0, ((0, 8), (1, 4))),
        "expert_ids": distinct(streams_of[1], TOKENS, EXPERTS, TOP, 8192),
        "gate_probs": jnp.clip(jnp.exp(math.log(0.6) - 2.4849067 * jax.random.uniform(streams_of[2], (TOKENS, TOP), jnp.float32) ** level_of(streams_of[2], (TOKENS, TOP), ((0, 8),), -0.2, 0.2)), 0.05, 0.6),
        "live": place_ends((jax.random.randint(streams_of[3], (TOKENS,), 0, 8) < 7).astype(jnp.int32), jax.random.fold_in(streams_of[3], 1), 0, 1),
        "w_gate": scatter_about(streams_of[4], (EXPERTS, FF, D), D ** -0.5, 0.09375, ((0, 8), (1, 4))),
        "w_up": scatter_about(streams_of[5], (EXPERTS, FF, D), D ** -0.5, 0.09375, ((0, 8), (1, 4))),
        "w_down": scatter_about(streams_of[6], (EXPERTS, FF, D), FF ** -0.5, 0.078125, ((0, 8), (1, 4))),
        "saved": scatter_about(streams_of[7], (EXPERTS, 2, FF, SLOTS), 1.5, 8.0, ((0, 8), (2, 4))),
    }


def reference(grad_out, expert_ids, gate_probs, live, w_gate, w_up, w_down, saved):
    groups = N_EXPERT
    experts = EXPERTS
    ids = expert_ids.reshape(groups, TOK_G * TOP)
    alive = jnp.repeat(live.reshape(groups, TOK_G), TOP, axis=1)
    onehot = (ids[:, :, None] == jnp.arange(experts, dtype=jnp.int32)[None, None, :]).astype(jnp.int32) * alive[:, :, None]
    position = jnp.sum((jnp.cumsum(onehot, axis=1) - onehot) * onehot, axis=2)
    kept = (jnp.sum(onehot, axis=2) > 0) & (position < CAP)
    group_index = jnp.arange(groups, dtype=jnp.int32)[:, None]
    place = ids * SLOTS + group_index * CAP + position
    place = jnp.where(kept, place, experts * SLOTS).astype(jnp.int32)
    scaled = (gate_probs.reshape(groups, TOK_G, TOP, 1) * grad_out.reshape(groups, TOK_G, 1, D).astype(jnp.float32)).astype(jnp.bfloat16)
    scaled = scaled.reshape(groups * TOK_G * TOP, D)
    buffer = jnp.zeros((experts * SLOTS + 1, D), jnp.bfloat16).at[place.reshape(-1)].set(scaled)
    buffer = buffer[: experts * SLOTS].reshape(experts, SLOTS, D)
    block_width = FF // N_TENSOR

    def one_expert(index):
        rows = buffer[index]
        grad_hidden = jnp.dot(w_down[index], rows.T, preferred_element_type=jnp.float32)
        pre_gate = saved[index, 0].astype(jnp.float32)
        pre_up = saved[index, 1].astype(jnp.float32)
        sigma = jax.nn.sigmoid(pre_gate)
        d_up = (grad_hidden * pre_gate * sigma).astype(jnp.bfloat16)
        d_gate = (grad_hidden * pre_up * sigma * (1.0 + pre_gate * (1.0 - sigma))).astype(jnp.bfloat16)
        gate_rows = w_gate[index]
        up_rows = w_up[index]

        def block(total, number):
            low = number * block_width
            gate_part = lax.dynamic_slice_in_dim(d_gate, low, block_width, 0)
            up_part = lax.dynamic_slice_in_dim(d_up, low, block_width, 0)
            gate_weights = lax.dynamic_slice_in_dim(gate_rows, low, block_width, 0)
            up_weights = lax.dynamic_slice_in_dim(up_rows, low, block_width, 0)
            term = jnp.dot(gate_part.T, gate_weights, preferred_element_type=jnp.float32)
            term = term + jnp.dot(up_part.T, up_weights, preferred_element_type=jnp.float32)
            rounded = lax.optimization_barrier(term.astype(jnp.bfloat16))
            return total + rounded.astype(jnp.float32), None

        total, _ = lax.scan(block, jnp.zeros((SLOTS, D), jnp.float32), jnp.arange(N_TENSOR, dtype=jnp.int32))
        return total

    slot_grad = lax.map(one_expert, jnp.arange(experts, dtype=jnp.int32))
    flat_rows = slot_grad.reshape(experts * SLOTS, D)
    picked = flat_rows[jnp.minimum(place, experts * SLOTS - 1).reshape(-1)]
    picked = picked * kept.reshape(-1, 1).astype(jnp.float32)
    grad_in = jnp.sum(picked.reshape(groups * TOK_G, TOP, D), axis=1)
    return grad_in.astype(jnp.bfloat16)
```

```python
import functools

import jax
import jax.numpy as jnp
from jax import lax
from jax.experimental import pallas as pl
from jax.experimental.pallas import tpu as pltpu
from jax.sharding import PartitionSpec as P

MESH = pl.DeviceIdType.MESH
NT = (((1,), (1,)), ((), ()))
NN = (((1,), (0,)), ((), ()))


def dot(a, b, dims):
    return lax.dot_general(a, b, dims, preferred_element_type=jnp.float32)


def mate(me, step, size, sign):
    if size & (size - 1):
        return lax.rem(me + (sign * step) % size, size)
    out, bit = 0, 1
    while bit < size:
        mine = lax.rem(lax.div(me, bit), 2)
        out = out + (1 - mine if step & bit else mine) * bit
        bit *= 2
    return out


def kernel(
    ne, nt, cap, raw0, ids, gates, live, w_gate, w_up, w_down, saved, out,
    wd, wg, wu, sv, svt, dh, sel, gs, back, outgoing, recv, orecv, raw, part, zrecv,
    w_sem, sv_sem, in_send, in_recv, out_send, out_recv, z_send, z_recv, p_send, p_recv,
):
    me = lax.axis_index("expert")
    mz = lax.axis_index("tensor")
    tokens, chunk = raw0.shape
    slots = ne * cap
    hidden = saved.shape[2]
    tops = ids.shape[0]
    steps = range(nt)
    owner = [mate(mz, s, nt, 1) for s in steps]
    zpeer = [mate(mz, s, nt, -1) for s in steps]
    order = sorted(range(1, ne), key=lambda j: (-(j // 2) if j > 1 else 1, j))
    epeer = [mate(me, j, ne, 1) for j in order]

    barrier = pltpu.get_barrier_semaphore()
    for peer in epeer:
        pl.semaphore_signal(barrier, inc=1, device_id=(peer, mz), device_id_type=MESH)
    for s in range(1, nt):
        pl.semaphore_signal(barrier, inc=1, device_id=(me, zpeer[s]), device_id_type=MESH)

    def weight_copy(i, s):
        src = (w_down, w_gate, w_up)[i]
        dst = (wd, wg, wu)[i]
        columns = pl.ds(pl.multiple_of(owner[s] * chunk, chunk), chunk)
        return pltpu.make_async_copy(src.at[0, :, columns], dst.at[s], w_sem.at[i, s])

    saved_copy = pltpu.make_async_copy(saved.at[0], sv, sv_sem.at[0])

    experts = lax.broadcasted_iota(jnp.int32, (ne, tokens), 0)
    alive = live[...] != 0
    chosen = jnp.zeros((ne, tokens), jnp.float32)
    weight = jnp.zeros((ne, tokens), jnp.float32)
    for k in range(tops):
        match = (ids[k : k + 1, :] == experts) & alive
        chosen = chosen + jnp.where(match, 1.0, 0.0)
        weight = weight + jnp.where(match, gates[k : k + 1, :], 0.0)
    row = lax.broadcasted_iota(jnp.int32, (tokens, tokens), 0)
    col = lax.broadcasted_iota(jnp.int32, (tokens, tokens), 1)
    before = jnp.where(row < col, 1.0, 0.0).astype(jnp.bfloat16)
    position = dot(chosen.astype(jnp.bfloat16), before, NN)
    position = jnp.where((chosen > 0.0) & (position < cap), position, -1.0)
    slot = lax.broadcasted_iota(jnp.int32, (cap, tokens), 0).astype(jnp.float32)
    for e in range(ne):
        hit = slot == position[e : e + 1, :]
        sel[e * cap : (e + 1) * cap, :] = jnp.where(hit, 1.0, 0.0).astype(jnp.bfloat16)
        gate = jnp.sum(jnp.where(hit, weight[e : e + 1, :], 0.0), axis=1, keepdims=True)
        gs[e * cap : (e + 1) * cap, :] = jnp.broadcast_to(gate, (cap, gs.shape[1]))

    tile = min(256, chunk)

    def build(src, s):
        @pl.loop(0, chunk // tile)
        def _(c):
            columns = pl.ds(pl.multiple_of(c * tile, tile), tile)
            picked = dot(sel[...], src[:, columns], NN)
            outgoing[s, :, columns] = (gs[:, :1] * picked).astype(jnp.bfloat16)

    def rows(e):
        return pl.ds(pl.multiple_of(e * cap, cap), cap)

    def exchange(s, dst, send, receive):
        for peer in epeer:
            pltpu.make_async_remote_copy(
                src_ref=outgoing.at[s, rows(peer)],
                dst_ref=dst.at[s, rows(me)],
                send_sem=send.at[s],
                recv_sem=receive.at[s],
                device_id=(peer, mz),
                device_id_type=MESH,
            ).start()
        pltpu.make_async_copy(
            outgoing.at[s, rows(me)], dst.at[s, rows(me)], receive.at[s]
        ).start()

    def wait_all(ref, sem):
        pltpu.make_async_copy(ref, ref, sem).wait()

    def z_copy(src, dst, s, send, receive, peer):
        return pltpu.make_async_remote_copy(
            src_ref=src,
            dst_ref=dst,
            send_sem=send.at[s],
            recv_sem=receive.at[s],
            device_id=(me, peer),
            device_id_type=MESH,
        )

    build(raw0, 0)
    pl.semaphore_wait(barrier, ne - 1 + nt - 1)
    z_copies = [
        z_copy(raw0, raw.at[s], s, z_send, z_recv, zpeer[s]) for s in range(1, nt)
    ]
    for copy in z_copies:
        copy.start()
    exchange(0, recv, in_send, in_recv)

    saved_copy.start()
    for s in steps:
        weight_copy(0, s).start()
    for s in reversed(steps):
        weight_copy(1, s).start()
        weight_copy(2, s).start()

    for s in range(1, nt):
        z_copies[s - 1].wait_recv()
        build(raw.at[s], s)
        exchange(s, recv, in_send, in_recv)

    row = lax.broadcasted_iota(jnp.int32, (tokens, tokens), 0)
    col = lax.broadcasted_iota(jnp.int32, (tokens, tokens), 1)
    eye = jnp.where(row == col, 1.0, 0.0).astype(jnp.bfloat16)
    back[...] = dot(eye, sel[...], NT).astype(jnp.bfloat16)
    block = min(128, slots)
    saved_copy.wait()

    @pl.loop(0, slots // block)
    def _(b):
        at = pl.ds(pl.multiple_of(b * block, block), block)
        r = lax.broadcasted_iota(jnp.int32, (block, block), 0)
        c = lax.broadcasted_iota(jnp.int32, (block, block), 1)
        one = jnp.where(r == c, 1.0, 0.0).astype(jnp.bfloat16)
        for i in range(2):
            svt[i, at, :] = dot(one, sv[i, :, at], NT).astype(jnp.bfloat16)

    half = min(256, slots)
    for s in steps:
        weight_copy(0, s).wait()
        wait_all(recv.at[s], in_recv.at[s])

        @pl.loop(0, slots // half)
        def _(b):
            at = pl.ds(pl.multiple_of(b * half, half), half)
            part_sum = dot(recv[s, at, :], wd[s], NT)
            if s == 0:
                dh[at, :] = part_sum
            else:
                dh[at, :] = dh[at, :] + part_sum

    few = 16

    @pl.loop(0, slots // few)
    def _(b):
        at = pl.ds(pl.multiple_of(b * few, few), few)
        grad = dh[at, :]
        a = svt[0, at, :].astype(jnp.float32)
        u = svt[1, at, :].astype(jnp.float32)
        sig = jax.nn.sigmoid(a)
        svt[1, at, :] = (grad * a * sig).astype(jnp.bfloat16)
        svt[0, at, :] = (grad * u * sig * (1.0 + a * (1.0 - sig))).astype(jnp.bfloat16)

    def combine(s, columns):
        return dot(back[...], orecv[s, :, columns], NN)

    p_copies = {
        s: z_copy(part.at[s], zrecv.at[s], s, p_send, p_recv, owner[s])
        for s in range(1, nt)
    }

    def finish(s):
        wait_all(orecv.at[s], out_recv.at[s])
        if s == 0:
            for q in range(1, nt):
                p_copies[q].wait_recv()

        @pl.loop(0, chunk // tile)
        def _(c):
            columns = pl.ds(pl.multiple_of(c * tile, tile), tile)
            total = combine(s, columns)
            if s == 0:
                for q in range(1, nt):
                    total = total + zrecv[q, :, columns].astype(jnp.float32)
                out[:, columns] = total.astype(jnp.bfloat16)
            else:
                part[s, :, columns] = total.astype(jnp.bfloat16)

        if s > 0:
            p_copies[s].start()

    others = outgoing.at[0, pl.ds(0, (ne - 1) * cap)]
    for s in reversed(steps):
        wait_all(others, in_send.at[s])
        weight_copy(1, s).wait()
        weight_copy(2, s).wait()

        @pl.loop(0, chunk // tile)
        def _(c):
            columns = pl.ds(pl.multiple_of(c * tile, tile), tile)
            term = dot(svt[0], wg[s, :, columns], NN)
            term = term + dot(svt[1], wu[s, :, columns], NN)
            outgoing[s, :, columns] = term.astype(jnp.bfloat16)

        exchange(s, orecv, out_send, out_recv)
    for s in reversed(steps):
        finish(s)

    for s in steps:
        wait_all(others, out_send.at[s])
    for s in range(1, nt):
        z_copies[s - 1].wait_send()
        p_copies[s].wait_send()


def shards(grad_out, expert_ids, gate_probs, live, w_gate, w_up, w_down, saved):
    ne = lax.axis_size("expert")
    nt = lax.axis_size("tensor")
    tokens, chunk = grad_out.shape
    cap = tokens * expert_ids.shape[1] // ne
    slots = ne * cap
    hidden = saved.shape[2]
    bf16, f32 = jnp.bfloat16, jnp.float32
    vmem = pl.BlockSpec(memory_space=pltpu.VMEM)
    anywhere = pl.BlockSpec(memory_space=pl.ANY)
    dma = pltpu.SemaphoreType.DMA
    return pl.pallas_call(
        functools.partial(kernel, ne, nt, cap),
        out_shape=jax.ShapeDtypeStruct((tokens, chunk), bf16),
        in_specs=[vmem] * 4 + [anywhere] * 4,
        out_specs=vmem,
        scratch_shapes=[
            pltpu.VMEM((nt, hidden, chunk), bf16),
            pltpu.VMEM((nt, hidden, chunk), bf16),
            pltpu.VMEM((nt, hidden, chunk), bf16),
            pltpu.VMEM((2, hidden, slots), bf16),
            pltpu.VMEM((2, slots, hidden), bf16),
            pltpu.VMEM((slots, hidden), f32),
            pltpu.VMEM((slots, tokens), bf16),
            pltpu.VMEM((slots, 128), f32),
            pltpu.VMEM((tokens, slots), bf16),
            pltpu.VMEM((nt, slots, chunk), bf16),
            pltpu.VMEM((nt, slots, chunk), bf16),
            pltpu.VMEM((nt, slots, chunk), bf16),
            pltpu.VMEM((nt, tokens, chunk), bf16),
            pltpu.VMEM((nt, tokens, chunk), bf16),
            pltpu.VMEM((nt, tokens, chunk), bf16),
            dma((3, nt)),
            dma((1,)),
            dma((nt,)),
            dma((nt,)),
            dma((nt,)),
            dma((nt,)),
            dma((nt,)),
            dma((nt,)),
            dma((nt,)),
            dma((nt,)),
        ],
        compiler_params=pltpu.CompilerParams(
            collective_id=0, has_side_effects=True, vmem_limit_bytes=67043328
        ),
    )(
        grad_out,
        expert_ids.T,
        gate_probs.T,
        live.reshape(1, tokens),
        w_gate,
        w_up,
        w_down,
        saved,
    )


def solution(mesh):
    placed = (
        P("expert", "tensor"),
        P("expert", None),
        P("expert", None),
        P("expert"),
        P("expert", "tensor", None),
        P("expert", "tensor", None),
        P("expert", "tensor", None),
        P("expert", None, "tensor", None),
    )
    return jax.shard_map(
        shards, mesh=mesh, in_specs=placed, out_specs=P("expert", "tensor"), check_vma=False
    )
```

```python
import functools

import jax
import jax.numpy as jnp
from jax import lax
from jax.experimental import pallas as pl
from jax.experimental.pallas import tpu as pltpu
from jax.sharding import PartitionSpec as P

MESH = pl.DeviceIdType.MESH
NT = (((1,), (1,)), ((), ()))
NN = (((1,), (0,)), ((), ()))
PARTS = 2


def dot(a, b, dims):
    return lax.dot_general(a, b, dims, preferred_element_type=jnp.float32)


def mate(me, step, size, sign):
    if size & (size - 1):
        return lax.rem(me + (sign * step) % size, size)
    out, bit = 0, 1
    while bit < size:
        mine = lax.rem(lax.div(me, bit), 2)
        out = out + (1 - mine if step & bit else mine) * bit
        bit *= 2
    return out


def kernel(
    ne, nt, cap, raw0, ids, gates, live, w_gate, w_up, w_down, saved, out,
    wd, wg, wu, sv, svt, dh, sel, gs, back, outgoing, recv, orecv, raw, part, zrecv,
    w_sem, sv_sem, in_send, in_recv, out_send, out_recv, z_send, z_recv, p_send, p_recv,
):
    me = lax.axis_index("expert")
    mz = lax.axis_index("tensor")
    tokens, chunk = raw0.shape
    few = cap // PARTS
    slots = ne * few
    tops = ids.shape[0]
    steps = range(nt)
    owner = [mate(mz, s, nt, 1) for s in steps]
    zpeer = [mate(mz, s, nt, -1) for s in steps]
    order = sorted(range(1, ne), key=lambda j: (-(j // 2) if j > 1 else 1, j))
    epeer = [mate(me, j, ne, 1) for j in order]

    barrier = pltpu.get_barrier_semaphore()
    for peer in epeer:
        pl.semaphore_signal(barrier, inc=1, device_id=(peer, mz), device_id_type=MESH)
    for s in range(1, nt):
        pl.semaphore_signal(barrier, inc=1, device_id=(me, zpeer[s]), device_id_type=MESH)

    def weight_copy(i, s):
        src = (w_down, w_gate, w_up)[i]
        dst = (wd, wg, wu)[i]
        columns = pl.ds(pl.multiple_of(owner[s] * chunk, chunk), chunk)
        return pltpu.make_async_copy(src.at[0, :, columns], dst.at[s], w_sem.at[i, s])

    saved_copy = pltpu.make_async_copy(saved.at[0], sv, sv_sem.at[0])

    experts = lax.broadcasted_iota(jnp.int32, (ne, tokens), 0)
    alive = live[...] != 0
    chosen = jnp.zeros((ne, tokens), jnp.float32)
    weight = jnp.zeros((ne, tokens), jnp.float32)
    for k in range(tops):
        match = (ids[k : k + 1, :] == experts) & alive
        chosen = chosen + jnp.where(match, 1.0, 0.0)
        weight = weight + jnp.where(match, gates[k : k + 1, :], 0.0)
    row = lax.broadcasted_iota(jnp.int32, (tokens, tokens), 0)
    col = lax.broadcasted_iota(jnp.int32, (tokens, tokens), 1)
    before = jnp.where(row < col, 1.0, 0.0).astype(jnp.bfloat16)
    position = dot(chosen.astype(jnp.bfloat16), before, NN)
    position = jnp.where((chosen > 0.0) & (position < cap), position, -1.0)
    slot = lax.broadcasted_iota(jnp.int32, (few, tokens), 0).astype(jnp.float32)
    for h in range(PARTS):
        for e in range(ne):
            at = slice(e * few, (e + 1) * few)
            hit = slot + float(h * few) == position[e : e + 1, :]
            sel[h, at, :] = jnp.where(hit, 1.0, 0.0).astype(jnp.bfloat16)
            gate = jnp.sum(jnp.where(hit, weight[e : e + 1, :], 0.0), axis=1, keepdims=True)
            gs[h, at, :] = jnp.broadcast_to(gate, (few, gs.shape[2]))

    tile = min(256, chunk)

    def build(src, h, s):
        @pl.loop(0, chunk // tile)
        def _(c):
            columns = pl.ds(pl.multiple_of(c * tile, tile), tile)
            picked = dot(sel[h], src[:, columns], NN)
            outgoing[h * nt + s, :, columns] = (gs[h, :, :1] * picked).astype(jnp.bfloat16)

    def rows(e):
        return pl.ds(pl.multiple_of(e * few, few), few)

    def exchange(s, dst, send, receive):
        for peer in epeer:
            pltpu.make_async_remote_copy(
                src_ref=outgoing.at[s, rows(peer)],
                dst_ref=dst.at[s, rows(me)],
                send_sem=send.at[s],
                recv_sem=receive.at[s],
                device_id=(peer, mz),
                device_id_type=MESH,
            ).start()
        pltpu.make_async_copy(
            outgoing.at[s, rows(me)], dst.at[s, rows(me)], receive.at[s]
        ).start()

    def wait_all(ref, sem):
        pltpu.make_async_copy(ref, ref, sem).wait()

    def z_copy(src, dst, s, send, receive, peer):
        return pltpu.make_async_remote_copy(
            src_ref=src,
            dst_ref=dst,
            send_sem=send.at[s],
            recv_sem=receive.at[s],
            device_id=(me, peer),
            device_id_type=MESH,
        )

    build(raw0, 0, 0)
    pl.semaphore_wait(barrier, ne - 1 + nt - 1)
    z_copies = [
        z_copy(raw0, raw.at[s], s, z_send, z_recv, zpeer[s]) for s in range(1, nt)
    ]
    for copy in z_copies:
        copy.start()
    exchange(0, recv, in_send, in_recv)

    saved_copy.start()
    for s in steps:
        weight_copy(0, s).start()
    for s in reversed(steps):
        weight_copy(1, s).start()
        weight_copy(2, s).start()

    def transpose_saved():
        saved_copy.wait()
        block = min(128, slots)
        for h in range(PARTS):

            @pl.loop(0, slots // block)
            def _(b):
                r = lax.broadcasted_iota(jnp.int32, (block, ne * cap), 0) + b * block
                c = lax.broadcasted_iota(jnp.int32, (block, ne * cap), 1)
                r = r.astype(jnp.float32)
                group = jnp.floor((r + 0.5) * (1.0 / few))
                place = r + group * float(cap - few) + float(h * few)
                one = jnp.where(place == c.astype(jnp.float32), 1.0, 0.0).astype(jnp.bfloat16)
                at = pl.ds(pl.multiple_of(b * block, block), block)
                for i in range(2):
                    svt[h, i, at, :] = dot(one, sv[i], NT).astype(jnp.bfloat16)

    units = [(0, s) for s in range(1, nt)] + [(h, s) for h in range(1, PARTS) for s in steps]
    if nt > 1:
        units.remove((1, 0))
        units.insert(1, (1, 0))
    for number, (h, s) in enumerate(units):
        if s > 0 and h == 0:
            z_copies[s - 1].wait_recv()
        build(raw.at[s] if s > 0 else raw0, h, s)
        exchange(h * nt + s, recv, in_send, in_recv)
        if number == 1:
            transpose_saved()

    row = lax.broadcasted_iota(jnp.int32, (tokens, tokens), 0)
    col = lax.broadcasted_iota(jnp.int32, (tokens, tokens), 1)
    eye = jnp.where(row == col, 1.0, 0.0).astype(jnp.bfloat16)
    for h in range(PARTS):
        back[h] = dot(eye, sel[h], NT).astype(jnp.bfloat16)

    others = outgoing.at[0, pl.ds(0, (ne - 1) * few)]

    def hidden_gradients(h):
        for s in steps:
            if h == 0:
                weight_copy(0, s).wait()
            wait_all(recv.at[h * nt + s], in_recv.at[h * nt + s])
            share = dot(recv[h * nt + s], wd[s], NT)
            if s == 0:
                dh[...] = share
            else:
                dh[...] = dh[...] + share

        thin = 16

        @pl.loop(0, slots // thin)
        def _(b):
            at = pl.ds(pl.multiple_of(b * thin, thin), thin)
            grad = dh[at, :]
            a = svt[h, 0, at, :].astype(jnp.float32)
            u = svt[h, 1, at, :].astype(jnp.float32)
            sig = jax.nn.sigmoid(a)
            svt[h, 1, at, :] = (grad * a * sig).astype(jnp.bfloat16)
            svt[h, 0, at, :] = (grad * u * sig * (1.0 + a * (1.0 - sig))).astype(jnp.bfloat16)

    def terms(h, s):
        unit = h * nt + s
        wait_all(others, in_send.at[unit])
        if h == 0:
            weight_copy(1, s).wait()
            weight_copy(2, s).wait()

        @pl.loop(0, chunk // tile)
        def _(c):
            columns = pl.ds(pl.multiple_of(c * tile, tile), tile)
            term = dot(svt[h, 0], wg[s, :, columns], NN)
            term = term + dot(svt[h, 1], wu[s, :, columns], NN)
            outgoing[unit, :, columns] = term.astype(jnp.bfloat16)

        exchange(unit, orecv, out_send, out_recv)

    def combine(s, columns):
        total = dot(back[0], orecv[s, :, columns], NN)
        for h in range(1, PARTS):
            total = total + dot(back[h], orecv[h * nt + s, :, columns], NN)
        return total

    p_copies = {
        s: z_copy(part.at[s], zrecv.at[s], s, p_send, p_recv, owner[s])
        for s in range(1, nt)
    }

    def finish(s):
        for h in range(PARTS):
            wait_all(orecv.at[h * nt + s], out_recv.at[h * nt + s])
        if s == 0:
            for q in range(1, nt):
                p_copies[q].wait_recv()

        @pl.loop(0, chunk // tile)
        def _(c):
            columns = pl.ds(pl.multiple_of(c * tile, tile), tile)
            total = combine(s, columns)
            if s == 0:
                for q in range(1, nt):
                    total = total + zrecv[q, :, columns].astype(jnp.float32)
                out[:, columns] = total.astype(jnp.bfloat16)
            else:
                part[s, :, columns] = total.astype(jnp.bfloat16)

        if s > 0:
            p_copies[s].start()

    for h in range(PARTS):
        hidden_gradients(h)
        for s in reversed(steps):
            terms(h, s)
    for s in reversed(steps):
        finish(s)

    for unit in range(PARTS * nt):
        wait_all(others, out_send.at[unit])
    for s in range(1, nt):
        z_copies[s - 1].wait_send()
        p_copies[s].wait_send()


def shards(grad_out, expert_ids, gate_probs, live, w_gate, w_up, w_down, saved):
    ne = lax.axis_size("expert")
    nt = lax.axis_size("tensor")
    tokens, chunk = grad_out.shape
    cap = tokens * expert_ids.shape[1] // ne
    slots = ne * cap
    part_slots = slots // PARTS
    hidden = saved.shape[2]
    bf16, f32 = jnp.bfloat16, jnp.float32
    vmem = pl.BlockSpec(memory_space=pltpu.VMEM)
    anywhere = pl.BlockSpec(memory_space=pl.ANY)
    dma = pltpu.SemaphoreType.DMA
    return pl.pallas_call(
        functools.partial(kernel, ne, nt, cap),
        out_shape=jax.ShapeDtypeStruct((tokens, chunk), bf16),
        in_specs=[vmem] * 4 + [anywhere] * 4,
        out_specs=vmem,
        scratch_shapes=[
            pltpu.VMEM((nt, hidden, chunk), bf16),
            pltpu.VMEM((nt, hidden, chunk), bf16),
            pltpu.VMEM((nt, hidden, chunk), bf16),
            pltpu.VMEM((2, hidden, slots), bf16),
            pltpu.VMEM((PARTS, 2, part_slots, hidden), bf16),
            pltpu.VMEM((part_slots, hidden), f32),
            pltpu.VMEM((PARTS, part_slots, tokens), bf16),
            pltpu.VMEM((PARTS, part_slots, 128), f32),
            pltpu.VMEM((PARTS, tokens, part_slots), bf16),
            pltpu.VMEM((PARTS * nt, part_slots, chunk), bf16),
            pltpu.VMEM((PARTS * nt, part_slots, chunk), bf16),
            pltpu.VMEM((PARTS * nt, part_slots, chunk), bf16),
            pltpu.VMEM((nt, tokens, chunk), bf16),
            pltpu.VMEM((nt, tokens, chunk), bf16),
            pltpu.VMEM((nt, tokens, chunk), bf16),
            dma((3, nt)),
            dma((1,)),
            dma((PARTS * nt,)),
            dma((PARTS * nt,)),
            dma((PARTS * nt,)),
            dma((PARTS * nt,)),
            dma((nt,)),
            dma((nt,)),
            dma((nt,)),
            dma((nt,)),
        ],
        compiler_params=pltpu.CompilerParams(
            collective_id=0, has_side_effects=True, vmem_limit_bytes=67043328
        ),
    )(
        grad_out,
        expert_ids.T,
        gate_probs.T,
        live.reshape(1, tokens),
        w_gate,
        w_up,
        w_down,
        saved,
    )


def solution(mesh):
    placed = (
        P("expert", "tensor"),
        P("expert", None),
        P("expert", None),
        P("expert"),
        P("expert", "tensor", None),
        P("expert", "tensor", None),
        P("expert", "tensor", None),
        P("expert", None, "tensor", None),
    )
    return jax.shard_map(
        shards, mesh=mesh, in_specs=placed, out_specs=P("expert", "tensor"), check_vma=False
    )
```

```python
import functools

import jax
import jax.numpy as jnp
from jax import lax
from jax.experimental import pallas as pl
from jax.experimental.pallas import tpu as pltpu
from jax.sharding import PartitionSpec as P

MESH = pl.DeviceIdType.MESH
NT = (((1,), (1,)), ((), ()))
NN = (((1,), (0,)), ((), ()))


def dot(a, b, dims):
    return lax.dot_general(a, b, dims, preferred_element_type=jnp.float32)


def mate(me, step, size, sign):
    if size & (size - 1):
        return lax.rem(me + (sign * step) % size, size)
    out, bit = 0, 1
    while bit < size:
        mine = lax.rem(lax.div(me, bit), 2)
        out = out + (1 - mine if step & bit else mine) * bit
        bit *= 2
    return out


def pieces_of(chunk):
    return chunk // 256 if chunk % 256 == 0 else 1


def kernel(
    ne, nt, cap, raw0, ids, gates, live, w_gate, w_up, w_down, saved, out,
    wd, wg, wu, sv, svt, dh, sel, gs, back, outgoing, recv, orecv, raw, part, zrecv,
    w_sem, sv_sem, in_send, in_recv, out_send, out_recv, z_send, z_recv, p_send, p_recv,
):
    me = lax.axis_index("expert")
    mz = lax.axis_index("tensor")
    tokens, chunk = raw0.shape
    slots = ne * cap
    hidden = saved.shape[2]
    tops = ids.shape[0]
    steps = range(nt)
    owner = [mate(mz, s, nt, 1) for s in steps]
    zpeer = [mate(mz, s, nt, -1) for s in steps]
    order = sorted(range(1, ne), key=lambda j: (-(j // 2) if j > 1 else 1, j))
    epeer = [mate(me, j, ne, 1) for j in order]

    barrier = pltpu.get_barrier_semaphore()
    for peer in epeer:
        pl.semaphore_signal(barrier, inc=1, device_id=(peer, mz), device_id_type=MESH)
    for s in range(1, nt):
        pl.semaphore_signal(barrier, inc=1, device_id=(me, zpeer[s]), device_id_type=MESH)

    def weight_copy(i, s):
        src = (w_down, w_gate, w_up)[i]
        dst = (wd, wg, wu)[i]
        columns = pl.ds(pl.multiple_of(owner[s] * chunk, chunk), chunk)
        return pltpu.make_async_copy(src.at[0, :, columns], dst.at[s], w_sem.at[i, s])

    saved_copy = pltpu.make_async_copy(saved.at[0], sv, sv_sem.at[0])

    experts = lax.broadcasted_iota(jnp.int32, (ne, tokens), 0)
    alive = live[...] != 0
    chosen = jnp.zeros((ne, tokens), jnp.float32)
    weight = jnp.zeros((ne, tokens), jnp.float32)
    for k in range(tops):
        match = (ids[k : k + 1, :] == experts) & alive
        chosen = chosen + jnp.where(match, 1.0, 0.0)
        weight = weight + jnp.where(match, gates[k : k + 1, :], 0.0)
    row = lax.broadcasted_iota(jnp.int32, (tokens, tokens), 0)
    col = lax.broadcasted_iota(jnp.int32, (tokens, tokens), 1)
    before = jnp.where(row < col, 1.0, 0.0).astype(jnp.bfloat16)
    position = dot(chosen.astype(jnp.bfloat16), before, NN)
    position = jnp.where((chosen > 0.0) & (position < cap), position, -1.0)
    slot = lax.broadcasted_iota(jnp.int32, (cap, tokens), 0).astype(jnp.float32)
    for e in range(ne):
        hit = slot == position[e : e + 1, :]
        sel[e * cap : (e + 1) * cap, :] = jnp.where(hit, 1.0, 0.0).astype(jnp.bfloat16)
        gate = jnp.sum(jnp.where(hit, weight[e : e + 1, :], 0.0), axis=1, keepdims=True)
        gs[e * cap : (e + 1) * cap, :] = jnp.broadcast_to(gate, (cap, gs.shape[1]))

    tile = min(256, chunk)
    pieces = pieces_of(chunk)
    width = chunk // pieces

    def build(src, s):
        @pl.loop(0, chunk // tile)
        def _(c):
            columns = pl.ds(pl.multiple_of(c * tile, tile), tile)
            picked = dot(sel[...], src[:, columns], NN)
            outgoing[s, :, columns] = (gs[:, :1] * picked).astype(jnp.bfloat16)

    def rows(e):
        return pl.ds(pl.multiple_of(e * cap, cap), cap)

    def exchange(s, dst, send, receive, sem=None, columns=pl.ds(0, chunk)):
        sem = s if sem is None else sem
        for peer in epeer:
            pltpu.make_async_remote_copy(
                src_ref=outgoing.at[s, rows(peer), columns],
                dst_ref=dst.at[s, rows(me), columns],
                send_sem=send.at[sem],
                recv_sem=receive.at[sem],
                device_id=(peer, mz),
                device_id_type=MESH,
            ).start()
        pltpu.make_async_copy(
            outgoing.at[s, rows(me), columns],
            dst.at[s, rows(me), columns],
            receive.at[sem],
        ).start()

    def wait_all(ref, sem):
        pltpu.make_async_copy(ref, ref, sem).wait()

    def z_copy(src, dst, s, send, receive, peer):
        return pltpu.make_async_remote_copy(
            src_ref=src,
            dst_ref=dst,
            send_sem=send.at[s],
            recv_sem=receive.at[s],
            device_id=(me, peer),
            device_id_type=MESH,
        )

    build(raw0, 0)
    pl.semaphore_wait(barrier, ne - 1 + nt - 1)
    z_copies = [
        z_copy(raw0, raw.at[s], s, z_send, z_recv, zpeer[s]) for s in range(1, nt)
    ]
    for copy in z_copies:
        copy.start()
    exchange(0, recv, in_send, in_recv)

    saved_copy.start()
    for s in steps:
        weight_copy(0, s).start()
    for s in reversed(steps):
        weight_copy(1, s).start()
        weight_copy(2, s).start()

    for s in range(1, nt):
        z_copies[s - 1].wait_recv()
        build(raw.at[s], s)
        exchange(s, recv, in_send, in_recv)

    row = lax.broadcasted_iota(jnp.int32, (tokens, tokens), 0)
    col = lax.broadcasted_iota(jnp.int32, (tokens, tokens), 1)
    eye = jnp.where(row == col, 1.0, 0.0).astype(jnp.bfloat16)
    back[...] = dot(eye, sel[...], NT).astype(jnp.bfloat16)
    block = min(128, slots)
    saved_copy.wait()

    @pl.loop(0, slots // block)
    def _(b):
        at = pl.ds(pl.multiple_of(b * block, block), block)
        r = lax.broadcasted_iota(jnp.int32, (block, block), 0)
        c = lax.broadcasted_iota(jnp.int32, (block, block), 1)
        one = jnp.where(r == c, 1.0, 0.0).astype(jnp.bfloat16)
        for i in range(2):
            svt[i, at, :] = dot(one, sv[i, :, at], NT).astype(jnp.bfloat16)

    half = min(256, slots)
    for s in steps:
        weight_copy(0, s).wait()
        wait_all(recv.at[s], in_recv.at[s])

        @pl.loop(0, slots // half)
        def _(b):
            at = pl.ds(pl.multiple_of(b * half, half), half)
            part_sum = dot(recv[s, at, :], wd[s], NT)
            if s == 0:
                dh[at, :] = part_sum
            else:
                dh[at, :] = dh[at, :] + part_sum

    few = 16

    @pl.loop(0, slots // few)
    def _(b):
        at = pl.ds(pl.multiple_of(b * few, few), few)
        grad = dh[at, :]
        a = svt[0, at, :].astype(jnp.float32)
        u = svt[1, at, :].astype(jnp.float32)
        sig = jax.nn.sigmoid(a)
        svt[1, at, :] = (grad * a * sig).astype(jnp.bfloat16)
        svt[0, at, :] = (grad * u * sig * (1.0 + a * (1.0 - sig))).astype(jnp.bfloat16)

    def combine(s, columns):
        return dot(back[...], orecv[s, :, columns], NN)

    p_copies = {
        s: z_copy(part.at[s], zrecv.at[s], s, p_send, p_recv, owner[s])
        for s in range(1, nt)
    }

    def finish(s):
        if s == 0:
            for q in range(1, nt):
                p_copies[q].wait_recv()
        for piece in range(pieces):
            here = pl.ds(piece * width, width)
            wait_all(orecv.at[s, :, here], out_recv.at[s * pieces + piece])

            @pl.loop(piece * (width // tile), (piece + 1) * (width // tile))
            def _(c):
                columns = pl.ds(pl.multiple_of(c * tile, tile), tile)
                total = combine(s, columns)
                if s == 0:
                    for q in range(1, nt):
                        total = total + zrecv[q, :, columns].astype(jnp.float32)
                    out[:, columns] = total.astype(jnp.bfloat16)
                else:
                    part[s, :, columns] = total.astype(jnp.bfloat16)

        if s > 0:
            p_copies[s].start()

    others = outgoing.at[0, pl.ds(0, (ne - 1) * cap)]
    for s in reversed(steps):
        wait_all(others, in_send.at[s])
        weight_copy(1, s).wait()
        weight_copy(2, s).wait()

        for piece in range(pieces):

            @pl.loop(piece * (width // tile), (piece + 1) * (width // tile))
            def _(c):
                columns = pl.ds(pl.multiple_of(c * tile, tile), tile)
                term = dot(svt[0], wg[s, :, columns], NN)
                term = term + dot(svt[1], wu[s, :, columns], NN)
                outgoing[s, :, columns] = term.astype(jnp.bfloat16)

            here = pl.ds(piece * width, width)
            exchange(s, orecv, out_send, out_recv, s * pieces + piece, here)
    for s in reversed(steps):
        finish(s)

    narrow = outgoing.at[0, pl.ds(0, (ne - 1) * cap), pl.ds(0, width)]
    for unit in range(nt * pieces):
        wait_all(narrow, out_send.at[unit])
    for s in range(1, nt):
        z_copies[s - 1].wait_send()
        p_copies[s].wait_send()


def shards(grad_out, expert_ids, gate_probs, live, w_gate, w_up, w_down, saved):
    ne = lax.axis_size("expert")
    nt = lax.axis_size("tensor")
    tokens, chunk = grad_out.shape
    cap = tokens * expert_ids.shape[1] // ne
    slots = ne * cap
    hidden = saved.shape[2]
    bf16, f32 = jnp.bfloat16, jnp.float32
    vmem = pl.BlockSpec(memory_space=pltpu.VMEM)
    anywhere = pl.BlockSpec(memory_space=pl.ANY)
    dma = pltpu.SemaphoreType.DMA
    return pl.pallas_call(
        functools.partial(kernel, ne, nt, cap),
        out_shape=jax.ShapeDtypeStruct((tokens, chunk), bf16),
        in_specs=[vmem] * 4 + [anywhere] * 4,
        out_specs=vmem,
        scratch_shapes=[
            pltpu.VMEM((nt, hidden, chunk), bf16),
            pltpu.VMEM((nt, hidden, chunk), bf16),
            pltpu.VMEM((nt, hidden, chunk), bf16),
            pltpu.VMEM((2, hidden, slots), bf16),
            pltpu.VMEM((2, slots, hidden), bf16),
            pltpu.VMEM((slots, hidden), f32),
            pltpu.VMEM((slots, tokens), bf16),
            pltpu.VMEM((slots, 128), f32),
            pltpu.VMEM((tokens, slots), bf16),
            pltpu.VMEM((nt, slots, chunk), bf16),
            pltpu.VMEM((nt, slots, chunk), bf16),
            pltpu.VMEM((nt, slots, chunk), bf16),
            pltpu.VMEM((nt, tokens, chunk), bf16),
            pltpu.VMEM((nt, tokens, chunk), bf16),
            pltpu.VMEM((nt, tokens, chunk), bf16),
            dma((3, nt)),
            dma((1,)),
            dma((nt,)),
            dma((nt,)),
            dma((nt * pieces_of(chunk),)),
            dma((nt * pieces_of(chunk),)),
            dma((nt,)),
            dma((nt,)),
            dma((nt,)),
            dma((nt,)),
        ],
        compiler_params=pltpu.CompilerParams(
            collective_id=0, has_side_effects=True, vmem_limit_bytes=67043328
        ),
    )(
        grad_out,
        expert_ids.T,
        gate_probs.T,
        live.reshape(1, tokens),
        w_gate,
        w_up,
        w_down,
        saved,
    )


def solution(mesh):
    placed = (
        P("expert", "tensor"),
        P("expert", None),
        P("expert", None),
        P("expert"),
        P("expert", "tensor", None),
        P("expert", "tensor", None),
        P("expert", "tensor", None),
        P("expert", None, "tensor", None),
    )
    return jax.shard_map(
        shards, mesh=mesh, in_specs=placed, out_specs=P("expert", "tensor"), check_vma=False
    )
```
